128 devices in a mesh: pipe: 8 (over x, core), role: 2 (over y_lo), tp: 8 (over z, y_hi).
Axes of the slice: x: 4, y: 4 (y_hi: 2, y_lo: 2; y = y_hi * 2 + y_lo), z: 4, core: 2. Of those that a mesh axis runs over, the one named last changes fastest.
Arguments:
- student_input: bfloat16 [512, 4096], P(('role', 'tp')), may hold values from -6 to 6
- teacher_hidden: bfloat16 [8, 512, 8192], P('pipe', None, ('role', 'tp')), may hold values from -40 to 40
- channel_order: int32 [8192], replicated, may hold values from 0 to 8191, each once
- norm_gain: float32 [8, 4096], P('pipe'), may hold values from 0.5 to 1.5
- w_gate: bfloat16 [8, 4096, 8192], P('pipe', None, ('role', 'tp')), may hold values from -0.09375 to 0.09375
- w_up: bfloat16 [8, 4096, 8192], P('pipe', None, ('role', 'tp')), may hold values from -0.09375 to 0.09375
- w_down: bfloat16 [8, 8192, 4096], P('pipe', ('role', 'tp')), may hold values from -0.0625 to 0.0625
Outputs:
- grad_gate: bfloat16 [8, 4096, 8192], P('pipe', None, ('role', 'tp'))
- grad_up: bfloat16 [8, 4096, 8192], P('pipe', None, ('role', 'tp'))
- grad_down: bfloat16 [8, 8192, 4096], P('pipe', ('role', 'tp'))
- grad_gain: float32 [8, 4096], P('pipe')
The draws below stay inside these ranges and needn't reach their ends.
Inputs may be any that keep to these rules, and one draw needn't show every extreme that they name: `channel_order`: a permutation; the first 4096 entries are the channels the student keeps.
All inputs are finite; a program needn't handle non-finite values.
Results may differ from the reference program's by a relative error of at most 0.017.
Values may be sent and summed in bfloat16 or wider, within the bound.
No kernel may reach another device: no remote copies, remote signals or barrier semaphores. Data moves between devices by JAX's collectives and lax.ppermute only.
A program may use at most 128 MiB of HBM per device.

```python
from functools import partial
import jax
import jax.numpy as jnp
from jax import lax

D = 4096
DT = 8192
FW = 8192
ROWS = 512
SECTIONS = 8
N_ROLE = 2
N_TP = 8


def draw_teacher_hidden(key, part):
    keys = jax.random.split(jax.random.fold_in(key, 7), 1)
    base = jax.random.normal(keys[0], (SECTIONS, ROWS, DT), jnp.float32)
    section_index = jnp.arange(SECTIONS).reshape(SECTIONS, 1, 1)
    step_weight = jnp.where(section_index == 0, 1.0, 0.3).astype(jnp.float32)
    values = jnp.cumsum(base * step_weight, axis=0)
    return jnp.clip(values, -40.0, 40.0).astype(jnp.bfloat16)


def block_levels(own_key, dims, cuts, least, high):
    gain, own = 1.0, jax.random.fold_in(own_key, 6)
    for dim, parts in cuts:
        draws = jnp.exp(jax.random.uniform(jax.random.fold_in(own, dim), (parts,), jnp.float32, least / len(cuts), high / len(cuts)))
        gain = gain * jnp.repeat(draws, dims[dim] // parts).reshape([-1 if axis == dim else 1 for axis in range(len(dims))])
    return gain


def gaussian(own_key, shape, spread, reach, pieces=(), dtype=jnp.bfloat16):
    values = spread * jax.random.normal(own_key, shape, jnp.float32)
    if pieces:
        values = values * block_levels(own_key, shape, pieces, -0.22, 0.18)
    return jnp.clip(values, -reach, reach).astype(dtype)


def setup_inputs(seed: int = 0) -> dict:
    seeds = jax.random.split(jax.random.key(seed), 8)
    return {
        "student_input": gaussian(seeds[0], (ROWS, D), 1.0, 6.0, ((0, 16),)),
        "teacher_hidden": draw_teacher_hidden(jax.random.fold_in(seeds[7], 71), 0),
        "channel_order": jax.random.permutation(seeds[2], DT).astype(jnp.int32),
        "norm_gain": jnp.clip(1.0 + 0.1 * jax.random.normal(seeds[3], (SECTIONS, D), jnp.float32), 0.5, 1.5),
        "w_gate": gaussian(seeds[4], (SECTIONS, D, FW), D ** -0.5, 0.09375, ((0, 8), (2, 16))),
        "w_up": gaussian(seeds[5], (SECTIONS, D, FW), D ** -0.5, 0.09375, ((0, 8), (2, 16))),
        "w_down": gaussian(seeds[6], (SECTIONS, FW, D), FW ** -0.5, 0.0625, ((0, 8), (1, 16))),
    }


epsilon = 1e-05

def one_section(operands, kept_channels):
    source, teacher, gain_row, weight_gate, weight_up, weight_down = operands
    groups = N_ROLE * N_TP
    source_f = source.astype(jnp.float32)
    inverse = lax.rsqrt(lax.optimization_barrier(jnp.mean(source_f * source_f, axis=1, keepdims=True)) + epsilon)
    normed = (source_f * inverse * gain_row).astype(jnp.bfloat16)
    gate_pre = jnp.dot(normed, weight_gate, preferred_element_type=jnp.float32)
    up_pre = jnp.dot(normed, weight_up, preferred_element_type=jnp.float32)
    gate_sig = jax.nn.sigmoid(gate_pre)
    hidden = (gate_pre * gate_sig * up_pre).astype(jnp.bfloat16)
    row_total = hidden.shape[0]
    per_group = hidden.shape[1] // groups
    hidden_groups = hidden.reshape(row_total, groups, per_group).astype(jnp.float32)
    down_groups = weight_down.reshape(groups, per_group, -1).astype(jnp.float32)
    group_terms = jnp.einsum('rgk,gkd->grd', hidden_groups, down_groups)
    group_terms = lax.optimization_barrier(group_terms.astype(jnp.bfloat16)).astype(jnp.float32)
    branch = lax.optimization_barrier(jnp.sum(group_terms, axis=0))
    output = source_f + branch
    out_inv = lax.rsqrt(lax.optimization_barrier(jnp.mean(output * output, axis=1, keepdims=True)) + epsilon)
    out_norm = output * out_inv
    teach_f = teacher.astype(jnp.float32)
    teach_inv = lax.rsqrt(lax.optimization_barrier(jnp.mean(teach_f * teach_f, axis=1, keepdims=True)) + epsilon)
    target = jnp.take(teach_f, kept_channels, axis=1) * teach_inv
    residue = out_norm - target
    out_grad = (out_inv * (residue - out_norm * lax.optimization_barrier(jnp.mean(residue * out_norm, axis=1, keepdims=True)))).astype(jnp.bfloat16)
    act_grad = jnp.dot(out_grad, weight_down.T, preferred_element_type=jnp.float32)
    gate_grad = (act_grad * up_pre * gate_sig * (1.0 + gate_pre * (1.0 - gate_sig))).astype(jnp.bfloat16)
    up_grad = (act_grad * gate_pre * gate_sig).astype(jnp.bfloat16)
    grad_down = jnp.dot(hidden.T, out_grad, preferred_element_type=jnp.float32).astype(jnp.bfloat16)
    grad_gate = jnp.dot(normed.T, gate_grad, preferred_element_type=jnp.float32).astype(jnp.bfloat16)
    grad_up = jnp.dot(normed.T, up_grad, preferred_element_type=jnp.float32).astype(jnp.bfloat16)
    gate_groups = gate_grad.reshape(row_total, groups, per_group).astype(jnp.float32)
    up_groups = up_grad.reshape(row_total, groups, per_group).astype(jnp.float32)
    wgate_groups = weight_gate.reshape(-1, groups, per_group).astype(jnp.float32)
    wup_groups = weight_up.reshape(-1, groups, per_group).astype(jnp.float32)
    normed_terms = jnp.einsum('rgk,dgk->grd', gate_groups, wgate_groups) + jnp.einsum('rgk,dgk->grd', up_groups, wup_groups)
    normed_terms = lax.optimization_barrier(normed_terms.astype(jnp.bfloat16)).astype(jnp.float32)
    normed_grad = lax.optimization_barrier(jnp.sum(normed_terms, axis=0))
    grad_gain = lax.optimization_barrier(jnp.sum(normed_grad * source_f * inverse, axis=0))
    return (grad_gate, grad_up, grad_down, grad_gain)

def reference(student_input, teacher_hidden, channel_order, norm_gain, w_gate, w_up, w_down):
    kept_channels = channel_order[:D].astype(jnp.int32)
    chosen = jnp.take(teacher_hidden[:-1], kept_channels, axis=2)
    sources = jnp.concatenate([student_input[None], chosen], axis=0)
    results = lax.map(partial(one_section, kept_channels=kept_channels), (sources, teacher_hidden, norm_gain, w_gate, w_up, w_down))
    return (results[0], results[1], results[2], results[3])
```

```python
import jax
import jax.numpy as jnp
from jax import lax
from jax.experimental import pallas as pl
from jax.experimental.pallas import tpu as pltpu
from jax.sharding import Mesh
from jax.sharding import PartitionSpec as P

GROUP = ("role", "tp_0", "tp_1")
epsilon = 1e-05
bf16 = jnp.bfloat16
f32 = jnp.float32


MASKS = {"y1": (1, 0), "y3": (3, 0), "z1": (0, 1), "z3": (0, 3)}


def exchange(block, mask):
    flip_y, flip_z = MASKS[mask]
    route = []
    for role in range(2):
        for z in range(4):
            for high in range(2):
                y = (high * 2 + role) ^ flip_y
                other = (y & 1) * 8 + (z ^ flip_z) * 2 + (y >> 1)
                route.append((role * 8 + z * 2 + high, other))
    return lax.ppermute(block, GROUP, route)


def joined(*blocks):
    return jnp.concatenate(blocks, axis=0)


def together(*blocks):
    return lax.optimization_barrier(blocks)


def plus(kept, arrived):
    return (kept.astype(f32) + arrived.astype(f32)).astype(bf16)


def gather_rows(a, b):
    at_a, at_b = exchange(a, "y1"), exchange(b, "z1")
    a, b = together(joined(a, at_a), joined(b, at_b))
    more_a, more_b = exchange(a, "y3"), exchange(b, "z3")
    side_a, side_b = exchange(a, "z1"), exchange(b, "y1")
    a, b, more_a, more_b = together(joined(a, side_a), joined(b, side_b), more_a, more_b)
    far_a, far_b = exchange(more_a, "z3"), exchange(more_b, "y3")
    a, b, more_a, more_b = together(a, b, joined(more_a, far_a), joined(more_b, far_b))
    early = (a, more_a, b, more_b)
    late = (exchange(a, "z3"), exchange(more_a, "z1"), exchange(b, "y3"), exchange(more_b, "y1"))
    return early, late


def scatter_rows(early, late):
    arrived = [exchange(block, mask) for block, mask in zip(late, ("z3", "z1", "y3", "y1"))]
    a, more_a, b, more_b = together(*[plus(kept, new) for kept, new in zip(early, arrived)])
    half = a.shape[0] // 2
    far_a, far_b = exchange(more_a[half:], "z3"), exchange(more_b[half:], "y3")
    side_a, side_b = exchange(a[half:], "z1"), exchange(b[half:], "y1")
    more_a, more_b, a, b = together(
        plus(more_a[:half], far_a), plus(more_b[:half], far_b), plus(a[:half], side_a), plus(b[:half], side_b)
    )
    new_a, new_b = exchange(more_a, "y3"), exchange(more_b, "z3")
    a, b = together(plus(a, new_a), plus(b, new_b))
    half = half // 2
    new_a, new_b = exchange(a[half:], "y1"), exchange(b[half:], "z1")
    return (
        a[:half].astype(f32) + new_a.astype(f32),
        b[:half].astype(f32) + new_b.astype(f32),
    )


def contract(left, right, left_dim, right_dim):
    return lax.dot_general(
        left, right, (((left_dim,), (right_dim,)), ((), ())), preferred_element_type=f32
    )


def take_body(order, blocks, out, turned, picked):
    step = pl.program_id(0)
    count = out.shape[1]
    width = blocks.shape[2]

    @pl.when(step == 0)
    def _():
        for k in range(blocks.shape[0]):
            turned[k * width : (k + 1) * width, :] = blocks[k].astype(f32).T

    for k in range(count):
        picked[k : k + 1, :] = turned[pl.ds(order[step * count + k], 1), :]
    out[...] = picked[...].T.astype(bf16)


def taken(blocks, order, width):
    sources, rows, channels = blocks.shape
    count = 512
    return pl.pallas_call(
        take_body,
        grid_spec=pltpu.PrefetchScalarGridSpec(
            num_scalar_prefetch=1,
            grid=(width // count,),
            in_specs=[pl.BlockSpec((sources, rows, channels), lambda i, _: (0, 0, 0))],
            out_specs=pl.BlockSpec((rows, count), lambda i, _: (0, i)),
            scratch_shapes=[
                pltpu.VMEM((sources * channels, rows), f32),
                pltpu.VMEM((count, rows), f32),
            ],
        ),
        out_shape=jax.ShapeDtypeStruct((rows, width), bf16),
        name="take_channels",
    )(order, blocks)


def weight_body(*refs):
    normed, gates, ups = refs[0:8], refs[8:10], refs[10:12]
    w_gate, w_up, out_gate, out_up, gain = refs[12:]
    rows = jnp.concatenate([ref[...] for ref in normed], axis=0)
    gate = contract(rows, jnp.concatenate([ref[...] for ref in gates], axis=0), 0, 0)
    up = contract(rows, jnp.concatenate([ref[...] for ref in ups], axis=0), 0, 0)
    out_gate[...] = gate.astype(bf16)
    out_up[...] = up.astype(bf16)
    product = gate * w_gate[...].astype(f32) + up * w_up[...].astype(f32)
    total = product[:, 0:128]
    for k in range(128, product.shape[1], 128):
        total = total + product[:, k : k + 128]
    gain[...] = jnp.sum(total.T, axis=0, keepdims=True)


def weight_grads(normed, gates, ups, w_gate, w_up):
    width, units = w_gate.shape
    count = 512
    across = lambda i: (0, i)
    down = lambda i: (i, 0)
    whole = lambda i: (0, 0)
    return pl.pallas_call(
        weight_body,
        grid=(width // count,),
        in_specs=[pl.BlockSpec((block.shape[0], count), across) for block in normed]
        + [pl.BlockSpec(block.shape, whole) for block in gates + ups]
        + [pl.BlockSpec((count, units), down)] * 2,
        out_specs=[pl.BlockSpec((count, units), down)] * 2 + [pl.BlockSpec((1, count), across)],
        out_shape=[jax.ShapeDtypeStruct((width, units), bf16)] * 2
        + [jax.ShapeDtypeStruct((1, width), f32)],
        name="weight_grads",
    )(*normed, *gates, *ups, w_gate, w_up)


def per_device(student_input, teacher_hidden, channel_order, norm_gain, w_gate, w_up, w_down):
    tokens, model_width = student_input.shape
    weight_gate = w_gate[0]
    weight_up = w_up[0]
    weight_down = w_down[0]
    gain_row = norm_gain[0]
    blocks = teacher_hidden[0].reshape(-1, tokens, teacher_hidden.shape[2])
    blocks = lax.all_to_all(blocks, GROUP, split_axis=0, concat_axis=0, tiled=True)
    chosen = taken(blocks, channel_order, model_width)
    stages = lax.axis_size("pipe")
    previous = lax.ppermute(chosen, "pipe", [(i, i + 1) for i in range(stages - 1)])
    source = jnp.where(lax.axis_index("pipe") == 0, student_input, previous)
    source_f = source.astype(f32)
    inverse = lax.rsqrt(jnp.mean(source_f * source_f, axis=1, keepdims=True) + epsilon)
    own_normed = (source_f * inverse * gain_row).astype(bf16)
    rows = tokens // 2
    normed = gather_rows(own_normed[:rows], own_normed[rows:])

    teach_f = blocks.astype(f32)
    teach_width = blocks.shape[0] * blocks.shape[2]
    teach_mean = jnp.sum(teach_f * teach_f, axis=(0, 2)) / teach_width
    target = chosen.astype(f32) * lax.rsqrt(teach_mean + epsilon)[:, None]

    saved, parts = [], []
    for pieces in normed:
        block = joined(*pieces)
        gate_pre = contract(block, weight_gate, 1, 0)
        up_pre = contract(block, weight_up, 1, 0)
        gate_sig = jax.nn.sigmoid(gate_pre)
        hidden = (gate_pre * gate_sig * up_pre).astype(bf16)
        saved.append((gate_pre, up_pre, gate_sig, hidden))
        branch = contract(hidden, weight_down, 1, 0).astype(bf16)
        parts.append(jnp.split(branch, 4, axis=0))
    branch_a, branch_b = scatter_rows(*parts)

    out_grads = []
    for k, branch in enumerate((branch_a, branch_b)):
        part = slice(k * rows, (k + 1) * rows)
        output = source_f[part] + branch
        out_inv = lax.rsqrt(jnp.mean(output * output, axis=1, keepdims=True) + epsilon)
        out_norm = output * out_inv
        residue = out_norm - target[part]
        slope = jnp.mean(residue * out_norm, axis=1, keepdims=True)
        out_grads.append((out_inv * (residue - out_norm * slope)).astype(bf16))
    grads = gather_rows(*out_grads)

    gate_grads, up_grads, full_grads = [], [], []
    for pieces, (gate_pre, up_pre, gate_sig, hidden) in zip(grads, saved):
        full_grad = joined(*pieces)
        act_grad = contract(full_grad, weight_down, 1, 1)
        gate_grads.append(
            (act_grad * up_pre * gate_sig * (1.0 + gate_pre * (1.0 - gate_sig))).astype(bf16)
        )
        up_grads.append((act_grad * gate_pre * gate_sig).astype(bf16))
        full_grads.append(full_grad)
    grad_gate, grad_up, gain_sum = weight_grads(
        normed[0] + normed[1], gate_grads, up_grads, weight_gate, weight_up
    )
    hidden = joined(*[item[3] for item in saved])
    grad_down = contract(hidden, joined(*full_grads), 0, 0).astype(bf16)
    gain_sum = gain_sum.reshape(-1, 128)
    for mask in ("y1", "z1", "y3", "z3"):
        gain_sum = gain_sum + exchange(gain_sum, mask)
    grad_gain = gain_sum.reshape(-1) / gain_row
    return grad_gate[None], grad_up[None], grad_down[None], grad_gain[None]


def solution(mesh):
    torus = Mesh(
        mesh.devices.reshape(mesh.shape["pipe"], mesh.shape["role"], 4, 2),
        ("pipe", "role", "tp_0", "tp_1"),
    )
    in_specs = (
        P(GROUP, None),
        P("pipe", None, GROUP),
        P(),
        P("pipe", None),
        P("pipe", None, GROUP),
        P("pipe", None, GROUP),
        P("pipe", GROUP, None),
    )
    out_specs = (
        P("pipe", None, GROUP),
        P("pipe", None, GROUP),
        P("pipe", GROUP, None),
        P("pipe", None),
    )
    return jax.shard_map(
        per_device, mesh=torus, in_specs=in_specs, out_specs=out_specs, check_vma=False
    )
```
